128 devices in a mesh: orig: 8 (over x, core), dest: 16 (over y, z).
Axes of the slice: x: 4, y: 4, z: 4, core: 2. Of those that a mesh axis runs over, the one named last changes fastest.
Arguments:
- root_blocks: bfloat16 [1024, 1024, 1024], P(('orig', 'dest')), may hold values from 0.0099487305 to 1
- sector_map: int32 [1024], replicated, may hold values from 0 to 127
- dest_owner: int32 [1024, 1], P(('orig', 'dest')), may hold values from 0 to 15; in each aligned block of 8 rows (0 to 7, 8 to 15, ...) at most 2 rows name the same one
- local_row: int32 [1024], P(('orig', 'dest')), may hold values from 0 to 7
- local_col: int32 [1024], P(('orig', 'dest')), may hold values from 0 to 3
- present: int32 [1024], P(('orig', 'dest')), may hold values 0 or 1
- prior: float32 [8192, 8192], P('orig', 'dest'), may hold values from 1 to 30
- row_target: float32 [8192], P('orig'), may hold values from 4096 to 16384
- col_target: float32 [8192], P('dest'), may hold values from 4096 to 16384
Outputs:
- balanced: float32 [8192, 8192], P('orig', 'dest')
The draws below stay inside these ranges and needn't reach their ends.
Inputs may be any that keep to these rules, and one draw needn't show every extreme that they name: Among the 8 root blocks of one device, no value of dest_owner occurs more than 2 times; some device has one that occurs exactly 2 times.
All inputs are finite; a program needn't handle non-finite values. No bound on the sum of `present` on one device may be relied on, other than what follows from the above.
Results may differ from the reference program's by a relative error of at most 0.0003.
Values sent between devices are 32-bit elements; how exact they have to be, the bound alone decides.
A program may use at most 128 MiB of HBM per device.

```python
import math
import jax
import jax.numpy as jnp
import numpy as np
from jax import lax

S_ROOT = 1024
S_T = 128
RB_DEV = 8
TRO = 8
CAP = 2
RB = 1024
TR = 64
TRD = 4
N_DEST = 16


def with_ends(entries, key, smallest, high):
    shape = entries.shape
    index_at = [jax.random.randint(jax.random.fold_in(key, axis), (), 0, shape[axis]) for axis in range(len(shape))]
    entries = entries.at[tuple(index_at)].set(smallest)
    longest = shape.index(max(shape))
    index_at[longest] = (index_at[longest] + 1) % shape[longest]
    return entries.at[tuple(index_at)].set(high)


def level_of(key, extent, pieces, low, high):
    level = 1.0
    for position, shards_of in pieces:
        draws = jax.random.uniform(jax.random.fold_in(jax.random.fold_in(key, 6), position), (shards_of,), jnp.float32, low / len(pieces), high / len(pieces))
        level = level * jnp.repeat(jnp.exp(draws), extent[position] // shards_of).reshape((-1,) + (1,) * (len(extent) - 1 - position))
    return level


def assign_block(own_key, own, number, rows, count, top, bound, slope):
    order = jax.random.permutation(own_key, count)
    packed, common = portions_of(count, rows * top, bound, slope, True), portions_of(count, rows * top, bound, slope, False)
    places = jnp.arange(count)

    def named(tallies, rotation):
        used = int((tallies > 0).sum())
        fixed = max(1, used // 4)
        passed = fixed + (places - fixed + rotation * (used - fixed)) % max(1, count - fixed)
        return jnp.zeros((count,), jnp.int32).at[order[jnp.where(places < fixed, places, passed)]].set(jnp.asarray(tallies, jnp.int32))

    tallies = jnp.where(number % 4 == 0, named(packed, number // 4), named(common, number - number // 4 - 1))
    mixed = jax.random.permutation(jax.random.fold_in(own, 3), count)
    source_of, taker = mixed[0:count // 2 * 2:2], mixed[1:count // 2 * 2:2]
    room = jnp.minimum(tallies[source_of] - 1, bound - tallies[taker]) // 2
    room = jnp.where((source_of == order[0]) | (taker == order[0]) | (tallies[taker] == 0), 0, jnp.maximum(room, 0))
    passed = jax.random.randint(jax.random.fold_in(own, 4), (count // 2,), 0, 1 << 20) % (room + 1)
    tallies = tallies.at[source_of].add(-passed).at[taker].add(passed)
    labels = jnp.searchsorted(jnp.cumsum(tallies), jnp.arange(rows * top), side="right").astype(jnp.int32)
    listing = labels.reshape(top, rows).T
    listing = listing[jax.random.permutation(jax.random.fold_in(own, 1), rows)]
    rotation = jax.random.randint(jax.random.fold_in(own, 2), (rows, 1), 0, top)
    return jnp.take_along_axis(listing, (jnp.arange(top)[None, :] + rotation) % top, axis=1)


def portions_of(amount, total, most, lean, full):
    portions = [(1 << 20) // math.isqrt(rank ** lean) + 1 for rank in range(1, amount + 1)]
    largest = most if full else min(most, max(-(-total // amount), total * portions[0] // sum(portions)))
    least = 1 if total - largest >= amount - 1 else 0
    given, spare = [largest] + [least] * (amount - 1), total - largest - least * (amount - 1)
    while spare > 0:
        candidates = [i for i in range(1, amount) if given[i] < largest] or [i for i in range(1, amount) if given[i] < most]
        whole, remaining = sum([portions[i] for i in candidates]), spare
        for i in candidates:
            addition = min(most - given[i], max(1, remaining * portions[i] // whole), spare)
            given[i] = given[i] + addition
            spare = spare - addition
    return np.array(given)


def setup_inputs(seed: int = 0) -> dict:
    streams_of = jax.random.split(jax.random.key(seed), 10)
    root_blocks = jnp.clip(jnp.exp(math.log(1.0) - 4.61031033 * jax.random.uniform(streams_of[0], (RB, S_ROOT, S_ROOT), jnp.float32) ** level_of(streams_of[0], (RB, S_ROOT, S_ROOT), ((0, 128),), -0.2, 0.2)), 0.0099487305, 1.0).astype(jnp.bfloat16)
    sector_map = with_ends(jax.random.randint(streams_of[1], (S_ROOT,), 0, S_T), jax.random.fold_in(streams_of[1], 1), 0, S_T - 1).astype(jnp.int32)
    dest_owner_keys = jax.random.split(jax.random.fold_in(streams_of[2], 1), RB // RB_DEV)
    dest_owner_turns = jax.random.permutation(jax.random.fold_in(streams_of[2], 3), RB // RB_DEV)
    dest_owner = jax.vmap(lambda own, number: assign_block(jax.random.fold_in(streams_of[2], 2), own, number, RB_DEV, N_DEST, 1, CAP, 2))(dest_owner_keys, dest_owner_turns).reshape((RB, 1))
    local_row = with_ends(jax.random.randint(streams_of[3], (RB,), 0, TRO), jax.random.fold_in(streams_of[3], 1), 0, TRO - 1).astype(jnp.int32)
    local_col = with_ends(jax.random.randint(streams_of[4], (RB,), 0, TRD), jax.random.fold_in(streams_of[4], 1), 0, TRD - 1).astype(jnp.int32)
    present = with_ends((jax.random.randint(streams_of[5], (RB,), 0, 4) < 3).astype(jnp.int32), jax.random.fold_in(streams_of[5], 1), 0, 1)
    prior = jnp.clip(jnp.exp(math.log(30.0) - 3.4011974 * jax.random.uniform(streams_of[6], (TR * S_T, TR * S_T), jnp.float32) ** level_of(streams_of[6], (TR * S_T, TR * S_T), ((0, 8), (1, 16)), -0.2, 0.2)), 1.0, 30.0)
    row_target = jnp.clip(jnp.exp(math.log(16384.0) - 1.3862944 * jax.random.uniform(streams_of[7], (TR * S_T,), jnp.float32) ** level_of(streams_of[7], (TR * S_T,), ((0, 8),), -0.2, 0.2)), 4096.0, 16384.0)
    col_target = jnp.clip(jnp.exp(math.log(16384.0) - 1.3862944 * jax.random.uniform(streams_of[8], (TR * S_T,), jnp.float32) ** level_of(streams_of[8], (TR * S_T,), ((0, 16),), -0.2, 0.2)), 4096.0, 16384.0)
    return dict(root_blocks=root_blocks, sector_map=sector_map, dest_owner=dest_owner, local_row=local_row, local_col=local_col, present=present, prior=prior, row_target=row_target, col_target=col_target)


def aggregate_one(block, concord, concord_wide):
    left = jnp.dot(concord.T, block, preferred_element_type=jnp.float32)
    return jnp.dot(left, concord_wide, preferred_element_type=jnp.float32, precision=lax.Precision.HIGHEST)


def reference(root_blocks, sector_map, dest_owner, local_row, local_col, present, prior, row_target, col_target):
    concord = (sector_map[:, None] == jnp.arange(S_T, dtype=jnp.int32)[None, :]).astype(jnp.bfloat16)
    concord_wide = concord.astype(jnp.float32)
    aggregated = lax.map(lambda blk: aggregate_one(blk, concord, concord_wide), root_blocks)
    aggregated = aggregated * present.astype(jnp.float32)[:, None, None]
    device = jnp.arange(RB, dtype=jnp.int32) // RB_DEV
    anchor_region = (device // N_DEST) * TRO + local_row
    dest_region = dest_owner[:, 0] * TRD + local_col
    tiles = prior.reshape(TR, S_T, TR, S_T).transpose(0, 2, 1, 3)
    tiles = tiles.at[anchor_region, dest_region].add(aggregated)
    table = tiles.transpose(0, 2, 1, 3).reshape(TR * S_T, TR * S_T)
    row_factor = row_target / jnp.sum(table, axis=1)
    scaled = table * row_factor[:, None]
    col_factor = col_target / jnp.sum(scaled, axis=0)
    return scaled * col_factor[None, :]
```

```python
import functools

import jax
import jax.numpy as jnp
from jax import lax
from jax.experimental import pallas as pl
from jax.experimental.pallas import tpu as pltpu
from jax.sharding import PartitionSpec as P

S_T = 128
HALF = S_T // 2
CAP = 2
SIDE = 4
MESH = pl.DeviceIdType.MESH
NT = (((1,), (1,)), ((), ()))
EXACT = lax.Precision.HIGHEST
F32 = jnp.float32
I32 = jnp.int32


def split(x):
    high = x.astype(jnp.bfloat16)
    return high, (x - high.astype(F32)).astype(jnp.bfloat16)


def route_kernel(
    sector_ref,
    owner,
    local_row,
    local_col,
    present,
    row_target,
    col_target,
    root,
    prior,
    got_a,
    got_b,
    meta_out,
    row_factor,
    col_factor,
    raw,
    concord_t,
    table,
    a_0,
    a_1,
    a_2,
    a_3,
    b_0,
    b_1,
    b_2,
    b_3,
    pack_a,
    pack_b,
    meta_v,
    meta_s,
    rows_1,
    rows_2,
    parts,
    cols_1,
    cols_2s,
    cols_2,
    cols_3,
    raw_sem,
    table_sem,
    meta_sem,
    gather_send,
    gather_recv,
    slot_send,
    slot_recv,
    keep_sem,
    small_send,
    small_recv,
    orig_send,
    orig_recv,
):
    from_a = (a_0, a_1, a_2, a_3)
    from_b = (b_0, b_1, b_2, b_3)
    n_blocks = root.shape[0]
    n_root = root.shape[1]
    n_orig = lax.axis_size("orig")
    tro = table.shape[0] // S_T
    trd = table.shape[1] // S_T
    o = lax.axis_index("orig")
    d = lax.axis_index("dest")
    y = d // SIDE
    z = d % SIDE

    def along_y(k):
        return (o, ((y + k) % SIDE) * SIDE + z)

    def along_z(k):
        return (o, y * SIDE + (z + k) % SIDE)

    def along_o(k):
        return ((o + k) % n_orig, d)

    def remote(src, dst, send, recv, device):
        return pltpu.make_async_remote_copy(
            src_ref=src, dst_ref=dst, send_sem=send, recv_sem=recv, device_id=device, device_id_type=MESH
        )

    def raw_copy(b):
        return pltpu.make_async_copy(root.at[b], raw.at[b], raw_sem.at[b])

    def start_raw(b, carry):
        raw_copy(b).start()
        return carry

    lax.fori_loop(0, n_blocks, start_raw, 0)
    table_copy = pltpu.make_async_copy(prior, table, table_sem)
    table_copy.start()

    barrier = pltpu.get_barrier_semaphore()
    for k in range(1, SIDE):
        pl.semaphore_signal(barrier, inc=1, device_id=along_y(k), device_id_type=MESH)
        pl.semaphore_signal(barrier, inc=1, device_id=along_z(k), device_id_type=MESH)
    for k in range(1, n_orig):
        pl.semaphore_signal(barrier, inc=1, device_id=along_o(k), device_id_type=MESH)

    target = lax.broadcasted_iota(I32, (S_T, S_T), 0)
    for c in range(n_root // S_T):
        concord_t[:, c * S_T : (c + 1) * S_T] = (target == sector_ref[c : c + 1, :]).astype(F32).astype(jnp.bfloat16)

    lane = lax.broadcasted_iota(I32, (1, S_T), 1)
    to = lane % 16
    kind = lane // 16
    none = jnp.full((1, S_T), tro * trd, I32)
    first = jnp.zeros((1, S_T), I32)
    second = jnp.zeros((1, S_T), I32)
    cell_1 = none
    cell_2 = none
    for b in reversed(range(n_blocks)):
        hit = to == owner[b, 0]
        second = jnp.where(hit, first, second)
        cell_2 = jnp.where(hit, cell_1, cell_2)
        first = jnp.where(hit, b, first)
        cell_1 = jnp.where(hit, local_row[b] * trd + local_col[b], cell_1)
    meta_v[z, y] = jnp.where(kind == 0, first, jnp.where(kind == 1, second, jnp.where(kind == 2, cell_1, cell_2)))

    pl.semaphore_wait(barrier, 2 * (SIDE - 1) + n_orig - 1)

    def small(i, k, src, dst, device):
        return remote(src, dst, small_send.at[i, k - 1], small_recv.at[i, k - 1], device)

    def meta_y(k):
        return small(0, k, meta_v.at[z, y], meta_v.at[z, y], along_y(k))

    def meta_z(k):
        return small(1, k, meta_v.at[z], meta_v.at[z], along_z(k))

    for k in range(1, SIDE):
        meta_y(k).start()

    def gather_copy(h, k, b):
        held, device = (from_a, along_y(k)) if h == 0 else (from_b, along_z(k))
        return remote(held[0].at[b], held[k].at[b], gather_send.at[h, k - 1, b], gather_recv.at[h, k - 1, b], device)

    sub = lax.broadcasted_iota(I32, (tro, S_T), 0)
    ones = jnp.ones((tro, S_T), F32)
    rows_1[y] = jnp.zeros((tro, S_T), F32)

    def aggregate(b, carry):
        raw_copy(b).wait()
        left = jnp.dot(concord_t[...], raw[b], preferred_element_type=F32)
        high, low = split(left)
        both = lax.dot_general(
            jnp.concatenate([high, low], axis=0), concord_t[...], NT, preferred_element_type=F32
        )
        block = (both[:S_T] + both[S_T:]) * present[b].astype(F32)
        a_0[b] = block[:HALF]
        b_0[b] = block[HALF:]
        for k in (2, 1, 3):
            gather_copy(0, k, b).start()
            gather_copy(1, k, b).start()
        sums = lax.dot_general(ones, block, NT, preferred_element_type=F32, precision=EXACT)
        rows_1[y] += jnp.where(sub == local_row[b], sums, 0.0)

        @pl.when(b == 2)
        def _():
            for k in range(1, SIDE):
                meta_y(k).wait()
            for k in range(1, SIDE):
                meta_z(k).start()

        return carry

    lax.fori_loop(0, n_blocks, aggregate, 0)

    for k in range(1, SIDE):
        meta_z(k).wait()
    meta_copy = pltpu.make_async_copy(meta_v, meta_s, meta_sem)
    meta_copy.start()
    meta_copy.wait()
    meta_out[...] = meta_v[...]

    def slot_copy(h, k, j):
        if h == 0:
            src, dst, device = pack_a.at[k, j], got_a.at[z, (y - j + SIDE) % SIDE], along_z(k)
        else:
            src, dst, device = pack_b.at[k, j], got_b.at[y, (z - j + SIDE) % SIDE], along_y(k)
        if k == 0:
            return pltpu.make_async_copy(src, dst, keep_sem.at[h, j])
        return remote(src, dst, slot_send.at[h, k - 1, j], slot_recv.at[h, k - 1, j], device)

    def fill(h, j):
        for k in (2, 1, 3, 0):
            for s in range(CAP):
                if h == 0:
                    source = (y - j + SIDE) % SIDE
                    index = meta_s[z, source, 0, y * SIDE + (z + k) % SIDE + 16 * s]
                    pack_a[k, j, s] = from_a[j][index]
                else:
                    source = (z - j + SIDE) % SIDE
                    index = meta_s[source, y, 0, ((y + k) % SIDE) * SIDE + z + 16 * s]
                    pack_b[k, j, s] = from_b[j][index]
            slot_copy(h, k, j).start()

    def arrived(j):
        def one(b, carry):
            gather_copy(0, j, b).wait_recv()
            gather_copy(1, j, b).wait_recv()
            return carry

        lax.fori_loop(0, n_blocks, one, 0)

    fill(0, 0)
    fill(1, 0)

    table_copy.wait()

    def prior_rows(r, carry):
        at = pl.multiple_of(r * S_T, S_T)
        tile = table[pl.ds(at, S_T), 0:S_T]
        for c in range(1, trd):
            tile += table[pl.ds(at, S_T), c * S_T : (c + 1) * S_T]
        sums = lax.dot_general(ones, tile, NT, preferred_element_type=F32, precision=EXACT)
        rows_1[y] += jnp.where(sub == r, sums, 0.0)
        return carry

    lax.fori_loop(0, tro, prior_rows, 0)

    def rows_y(k):
        return small(2, k, rows_1.at[y], rows_1.at[y], along_y(k))

    def rows_z(k):
        return small(3, k, rows_2.at[z], rows_2.at[z], along_z(k))

    for k in range(1, SIDE):
        rows_y(k).start()
    arrived(1)
    fill(0, 1)
    fill(1, 1)
    for k in range(1, SIDE):
        rows_y(k).wait()
    rows_2[z] = (rows_1[0] + rows_1[1]) + (rows_1[2] + rows_1[3])
    for k in range(1, SIDE):
        rows_z(k).start()
    arrived(3)
    fill(0, 3)
    fill(1, 3)
    for k in range(1, SIDE):
        rows_z(k).wait()
    factor = row_target[...] / ((rows_2[0] + rows_2[1]) + (rows_2[2] + rows_2[3]))
    row_factor[...] = factor

    parts[...] = jnp.zeros_like(parts)
    place = lax.broadcasted_iota(I32, parts.shape, 0) * trd + lax.broadcasted_iota(I32, parts.shape, 1)

    def block_cols(b, carry):
        weight = jnp.where(sub == local_row[b], factor, 0.0)
        sums = jnp.dot(weight[:, :HALF], a_0[b], preferred_element_type=F32, precision=EXACT) + jnp.dot(
            weight[:, HALF:], b_0[b], preferred_element_type=F32, precision=EXACT
        )
        line = jnp.sum(sums, axis=0, keepdims=True)
        here = place == owner[b, 0] * trd + local_col[b]
        parts[...] += jnp.where(here, jnp.broadcast_to(line[None], parts.shape), 0.0)
        return carry

    lax.fori_loop(0, n_blocks, block_cols, 0)

    def cols_y(k):
        return small(4, k, parts.at[pl.ds(((y + k) % SIDE) * SIDE, SIDE)], cols_1.at[y], along_y(k))

    def cols_z(k):
        return small(5, k, cols_2s.at[(z + k) % SIDE], cols_2.at[z], along_z(k))

    for k in range(1, SIDE):
        cols_y(k).start()
    cols_1[y] = parts[pl.ds(y * SIDE, SIDE)]
    arrived(2)
    fill(0, 2)
    fill(1, 2)

    def prior_cols(r, carry):
        at = pl.multiple_of(r * S_T, S_T)
        weight = jnp.where(sub == r, factor, 0.0)
        return carry + jnp.dot(weight, table[pl.ds(at, S_T), :], preferred_element_type=F32, precision=EXACT)

    wide = lax.fori_loop(0, tro, prior_cols, jnp.zeros((tro, trd * S_T), F32))
    wide = jnp.sum(wide, axis=0, keepdims=True)

    for k in range(1, SIDE):
        cols_y(k).wait()
    cols_2s[...] = (cols_1[0] + cols_1[1]) + (cols_1[2] + cols_1[3])
    for k in range(1, SIDE):
        cols_z(k).start()
    cols_2[z] = cols_2s[z]
    for k in range(1, SIDE):
        cols_z(k).wait()
    moved = (cols_2[0] + cols_2[1]) + (cols_2[2] + cols_2[3])
    for c in range(trd):
        cols_3[o, c : c + 1, :] = moved[c : c + 1, :] + wide[:, c * S_T : (c + 1) * S_T]

    def cols_o(k):
        return remote(cols_3.at[o], cols_3.at[o], orig_send.at[k - 1], orig_recv.at[k - 1], along_o(k))

    for k in range(1, n_orig):
        cols_o(k).start()
    for k in range(1, n_orig):
        cols_o(k).wait()
    total = cols_3[0]
    for i in range(1, n_orig):
        total += cols_3[i]
    col_factor[...] = col_target[...] / total

    def sent(b, carry):
        for k in range(1, SIDE):
            gather_copy(0, k, b).wait_send()
            gather_copy(1, k, b).wait_send()
        return carry

    lax.fori_loop(0, n_blocks, sent, 0)
    for j in (0, 1, 3, 2):
        for k in (0, 1, 3, 2):
            slot_copy(0, k, j).wait()
            slot_copy(1, k, j).wait()


def place_kernel(meta, row_factor, col_factor, got_a, got_b, prior, out, table, slots_a, slots_b, sem, out_sem):
    trd = table.shape[1] // S_T
    tro = table.shape[0] // S_T
    me = lax.axis_index("dest")
    copies = [
        pltpu.make_async_copy(prior, table, sem.at[0]),
        pltpu.make_async_copy(got_a, slots_a, sem.at[1]),
        pltpu.make_async_copy(got_b, slots_b, sem.at[2]),
    ]
    for copy in copies:
        copy.start()
    for copy in copies:
        copy.wait()

    def add(i, carry):
        ys = i // SIDE
        zs = i % SIDE
        for s in range(CAP):
            cell = meta[zs, ys, 0, me + 16 * (2 + s)]

            @pl.when(cell < tro * trd)
            def _():
                at = pl.multiple_of((cell // trd) * S_T, S_T)
                col = pl.multiple_of((cell % trd) * S_T, S_T)
                table[pl.ds(at, HALF), pl.ds(col, S_T)] += slots_a[zs, ys, s]
                table[pl.ds(at + HALF, HALF), pl.ds(col, S_T)] += slots_b[ys, zs, s]

        return carry

    lax.fori_loop(0, SIDE * SIDE, add, 0)

    def out_copy(r):
        at = pl.multiple_of(r * S_T, S_T)
        return pltpu.make_async_copy(table.at[pl.ds(at, S_T)], out.at[pl.ds(at, S_T)], out_sem.at[r])

    for r in range(tro):
        scale = jnp.transpose(jnp.broadcast_to(row_factor[r : r + 1, :], (S_T, S_T)))
        for c in range(trd):
            where = (slice(r * S_T, (r + 1) * S_T), slice(c * S_T, (c + 1) * S_T))
            table[where] = (scale * table[where]) * col_factor[c : c + 1, :]
        out_copy(r).start()
    for r in range(tro):
        out_copy(r).wait()


def shards(
    root_blocks,
    sector_map,
    dest_owner,
    local_row,
    local_col,
    present,
    prior,
    row_target,
    col_target,
):
    n_blocks, n_root, _ = root_blocks.shape
    rows_here, cols_here = prior.shape
    tro = rows_here // S_T
    trd = cols_here // S_T
    n_orig = lax.axis_size("orig")
    vmem = pl.BlockSpec(memory_space=pltpu.VMEM)
    smem = pl.BlockSpec(memory_space=pltpu.SMEM)
    hbm = pl.BlockSpec(memory_space=pl.ANY)
    dma = pltpu.SemaphoreType.DMA
    got = jax.ShapeDtypeStruct((SIDE, SIDE, CAP, HALF, S_T), F32)
    got_a, got_b, meta, row_factor, col_factor = pl.pallas_call(
        route_kernel,
        out_shape=(
            got,
            got,
            jax.ShapeDtypeStruct((SIDE, SIDE, 1, S_T), I32),
            jax.ShapeDtypeStruct((tro, S_T), F32),
            jax.ShapeDtypeStruct((trd, S_T), F32),
        ),
        in_specs=[vmem, smem, smem, smem, smem, vmem, vmem, hbm, hbm],
        out_specs=(hbm, hbm, vmem, vmem, vmem),
        scratch_shapes=[
            pltpu.VMEM((n_blocks, n_root, n_root), jnp.bfloat16),
            pltpu.VMEM((S_T, n_root), jnp.bfloat16),
            pltpu.VMEM((rows_here, cols_here), F32),
            *[pltpu.VMEM((n_blocks, HALF, S_T), F32)] * (2 * SIDE),
            pltpu.VMEM((SIDE, SIDE, CAP, HALF, S_T), F32),
            pltpu.VMEM((SIDE, SIDE, CAP, HALF, S_T), F32),
            pltpu.VMEM((SIDE, SIDE, 1, S_T), I32),
            pltpu.SMEM((SIDE, SIDE, 1, S_T), I32),
            pltpu.VMEM((SIDE, tro, S_T), F32),
            pltpu.VMEM((SIDE, tro, S_T), F32),
            pltpu.VMEM((SIDE * SIDE, trd, S_T), F32),
            pltpu.VMEM((SIDE, SIDE, trd, S_T), F32),
            pltpu.VMEM((SIDE, trd, S_T), F32),
            pltpu.VMEM((SIDE, trd, S_T), F32),
            pltpu.VMEM((n_orig, trd, S_T), F32),
            dma((n_blocks,)),
            dma,
            dma,
            dma((2, SIDE - 1, n_blocks)),
            dma((2, SIDE - 1, n_blocks)),
            dma((2, SIDE - 1, SIDE)),
            dma((2, SIDE - 1, SIDE)),
            dma((2, SIDE)),
            dma((6, SIDE - 1)),
            dma((6, SIDE - 1)),
            dma((n_orig - 1,)),
            dma((n_orig - 1,)),
        ],
        compiler_params=pltpu.CompilerParams(
            collective_id=0, has_side_effects=True, vmem_limit_bytes=48 << 20
        ),
        name="route",
    )(
        sector_map.reshape(n_root // S_T, S_T),
        dest_owner,
        local_row,
        local_col,
        present,
        row_target.reshape(tro, S_T),
        col_target.reshape(trd, S_T),
        root_blocks,
        prior,
    )
    return pl.pallas_call(
        place_kernel,
        out_shape=jax.ShapeDtypeStruct((rows_here, cols_here), F32),
        in_specs=[smem, vmem, vmem, hbm, hbm, hbm],
        out_specs=hbm,
        scratch_shapes=[
            pltpu.VMEM((rows_here, cols_here), F32),
            pltpu.VMEM((SIDE, SIDE, CAP, HALF, S_T), F32),
            pltpu.VMEM((SIDE, SIDE, CAP, HALF, S_T), F32),
            dma((3,)),
            dma((tro,)),
        ],
        compiler_params=pltpu.CompilerParams(vmem_limit_bytes=24 << 20),
        name="place",
    )(meta, row_factor, col_factor, got_a, got_b, prior)


def solution(mesh):
    placed = (
        P(("orig", "dest"), None, None),
        P(),
        P(("orig", "dest"), None),
        P(("orig", "dest")),
        P(("orig", "dest")),
        P(("orig", "dest")),
        P("orig", "dest"),
        P("orig"),
        P("dest"),
    )
    return jax.shard_map(
        shards, mesh=mesh, in_specs=placed, out_specs=P("orig", "dest"), check_vma=False
    )
```

```python
import functools

import jax
import jax.numpy as jnp
from jax import lax
from jax.experimental import pallas as pl
from jax.experimental.pallas import tpu as pltpu
from jax.sharding import PartitionSpec as P

S_T = 128
HALF = S_T // 2
CAP = 2
SIDE = 4
LAG = 5
LATE = 5
MESH = pl.DeviceIdType.MESH
NT = (((1,), (1,)), ((), ()))
F32 = jnp.float32
I32 = jnp.int32


def split(x):
    high = x.astype(jnp.bfloat16)
    return high, (x - high.astype(F32)).astype(jnp.bfloat16)


def route_kernel(
    sector_hbm,
    owner_hbm,
    local_row_hbm,
    local_col_hbm,
    present_hbm,
    row_target_hbm,
    col_target_hbm,
    root,
    prior,
    got_a,
    got_b,
    meta_out,
    weights,
    table,
    col_factor,
    sector_ref,
    owner,
    local_row,
    local_col,
    present,
    row_target,
    col_target,
    raw,
    concord_t,
    a_0,
    a_1,
    a_2,
    a_3,
    b_0,
    b_1,
    b_2,
    b_3,
    pack_a,
    pack_b,
    meta_v,
    meta_s,
    row_acc,
    rows,
    cols_a,
    cols_b,
    cols_all,
    small_sem,
    raw_sem,
    table_sem,
    meta_sem,
    gather_send,
    gather_recv,
    pass_send,
    pass_recv,
    slot_send,
    slot_recv,
    keep_sem,
    small_send,
    small_recv,
    rows_send,
    rows_recv,
    cols_send,
    cols_recv,
    orig_send,
    orig_recv,
):
    from_a = (a_0, a_1, a_2, a_3)
    from_b = (b_0, b_1, b_2, b_3)
    n_blocks = root.shape[0]
    n_root = root.shape[1]
    n_orig = lax.axis_size("orig")
    n_dest = lax.axis_size("dest")
    tro = table.shape[0] // S_T
    trd = table.shape[1] // S_T
    o = lax.axis_index("orig")
    d = lax.axis_index("dest")
    y = d // SIDE
    z = d % SIDE

    def along_y(k):
        return (o, ((y + k) % SIDE) * SIDE + z)

    def along_z(k):
        return (o, y * SIDE + (z + k) % SIDE)

    def along_d(i):
        return (o, (d + i) % n_dest)

    def along_o(k):
        return ((o + k) % n_orig, d)

    def remote(src, dst, send, recv, device):
        return pltpu.make_async_remote_copy(
            src_ref=src, dst_ref=dst, send_sem=send, recv_sem=recv, device_id=device, device_id_type=MESH
        )

    def raw_copy(b):
        return pltpu.make_async_copy(root.at[b], raw.at[b], raw_sem.at[b])

    barrier = pltpu.get_barrier_semaphore()
    for k in range(1, SIDE):
        pl.semaphore_signal(barrier, inc=1, device_id=along_y(k), device_id_type=MESH)
        pl.semaphore_signal(barrier, inc=1, device_id=along_z(k), device_id_type=MESH)
    for k in range(1, n_orig):
        pl.semaphore_signal(barrier, inc=1, device_id=along_o(k), device_id_type=MESH)

    loads = [
        pltpu.make_async_copy(src, dst, small_sem.at[i])
        for i, (src, dst) in enumerate(
            (
                (sector_hbm, sector_ref),
                (owner_hbm, owner),
                (local_row_hbm, local_row),
                (local_col_hbm, local_col),
                (present_hbm, present),
                (row_target_hbm, row_target),
                (col_target_hbm, col_target),
            )
        )
    ]
    for load in loads:
        load.start()

    def start_raw(b, carry):
        raw_copy(b).start()
        return carry

    lax.fori_loop(0, n_blocks, start_raw, 0)
    table_copy = pltpu.make_async_copy(prior, table, table_sem)

    for load in loads:
        load.wait()

    target = lax.broadcasted_iota(I32, (S_T, S_T), 0)
    for c in range(n_root // S_T):
        concord_t[:, c * S_T : (c + 1) * S_T] = (target == sector_ref[c : c + 1, :]).astype(F32).astype(jnp.bfloat16)

    lane = lax.broadcasted_iota(I32, (1, S_T), 1)
    to = lane % 16
    kind = lane // 16
    none = jnp.full((1, S_T), tro * trd, I32)
    first = jnp.zeros((1, S_T), I32)
    second = jnp.zeros((1, S_T), I32)
    cell_1 = none
    cell_2 = none
    for b in reversed(range(n_blocks)):
        hit = to == owner[0, b]
        second = jnp.where(hit, first, second)
        cell_2 = jnp.where(hit, cell_1, cell_2)
        first = jnp.where(hit, b, first)
        cell_1 = jnp.where(hit, local_row[0, b] * trd + local_col[0, b], cell_1)
    meta_v[z, y] = jnp.where(kind == 0, first, jnp.where(kind == 1, second, jnp.where(kind == 2, cell_1, cell_2)))

    pl.semaphore_wait(barrier, 2 * (SIDE - 1) + n_orig - 1)

    def small(i, k, src, dst, device):
        return remote(src, dst, small_send.at[i, k - 1], small_recv.at[i, k - 1], device)

    def meta_y(k):
        return small(0, k, meta_v.at[z, y], meta_v.at[z, y], along_y(k))

    def meta_z(k):
        return small(1, k, meta_v.at[z], meta_v.at[z], along_z(k))

    for k in range(1, SIDE):
        meta_y(k).start()

    def gather_copy(h, k, b):
        held, device = (from_a, along_y(k)) if h == 0 else (from_b, along_z(k))
        return remote(held[0].at[b], held[k].at[b], gather_send.at[h, k - 1, b], gather_recv.at[h, k - 1, b], device)

    def pass_copy(h, way, b):
        held = from_a if h == 0 else from_b
        along = along_y if h == 0 else along_z
        piece = pl.ds(0, HALF // 2) if way == 0 else pl.ds(HALF // 2, HALF // 2)
        source, k = (1, 1) if way == 0 else (3, 3)
        return remote(
            held[source].at[b, piece],
            held[2].at[b, piece],
            pass_send.at[h, way, b],
            pass_recv.at[h, way, b],
            along(k),
        )

    def forward(b):
        for way, k in ((0, 1), (1, 3)):
            for h in (0, 1):
                gather_copy(h, k, b).wait_recv()
                pass_copy(h, way, b).start()

    lanes = lax.broadcasted_iota(I32, (S_T, S_T), 1)
    row_acc[...] = jnp.zeros_like(row_acc)

    def aggregate(b, carry):
        raw_copy(b).wait()

        @pl.when(b == LATE)
        def _():
            table_copy.start()

        left = jnp.dot(concord_t[...], raw[b], preferred_element_type=F32)
        high, low = split(left)
        both = lax.dot_general(
            jnp.concatenate([high, low], axis=0), concord_t[...], NT, preferred_element_type=F32
        )
        block = (both[:S_T] + both[S_T:]) * present[0, b].astype(F32)
        a_0[b] = block[:HALF]
        b_0[b] = block[HALF:]
        for k in (1, 3):
            gather_copy(0, k, b).start()
            gather_copy(1, k, b).start()

        @pl.when(b >= LAG)
        def _():
            forward(b - LAG)

        sums = jnp.sum(block, axis=1, keepdims=True)
        row_acc[...] += jnp.where(lanes == local_row[0, b], sums, 0.0)

        @pl.when(b == 2)
        def _():
            for k in range(1, SIDE):
                meta_y(k).wait()
            for k in range(1, SIDE):
                meta_z(k).start()

        return carry

    lax.fori_loop(0, n_blocks, aggregate, 0)

    table_copy.wait()

    def prior_rows(r, carry):
        at = pl.multiple_of(r * S_T, S_T)
        tile = table[pl.ds(at, S_T), 0:S_T]
        for c in range(1, trd):
            tile += table[pl.ds(at, S_T), c * S_T : (c + 1) * S_T]
        row_acc[...] += jnp.where(lanes == r, jnp.sum(tile, axis=1, keepdims=True), 0.0)
        return carry

    lax.fori_loop(0, tro, prior_rows, 0)
    rows[d] = jnp.transpose(row_acc[...])[:tro]

    def rows_copy(i):
        return remote(rows.at[d], rows.at[d], rows_send.at[i - 1], rows_recv.at[i - 1], along_d(i))

    def start_rows(i, carry):
        rows_copy(i).start()
        return carry

    lax.fori_loop(1, n_dest, start_rows, 0)

    for k in range(1, SIDE):
        meta_z(k).wait()
    meta_copy = pltpu.make_async_copy(meta_v, meta_s, meta_sem)
    meta_copy.start()
    meta_copy.wait()
    meta_out[...] = meta_v[...]

    def slot_copy(h, k, j):
        if h == 0:
            src, dst, device = pack_a.at[k, j], got_a.at[z, (y - j + SIDE) % SIDE], along_z(k)
        else:
            src, dst, device = pack_b.at[k, j], got_b.at[y, (z - j + SIDE) % SIDE], along_y(k)
        if k == 0:
            return pltpu.make_async_copy(src, dst, keep_sem.at[h, j])
        return remote(src, dst, slot_send.at[h, k - 1, j], slot_recv.at[h, k - 1, j], device)

    def fill(h, j):
        for k in (2, 1, 3, 0):
            for s in range(CAP):
                if h == 0:
                    source = (y - j + SIDE) % SIDE
                    index = meta_s[z, source, 0, y * SIDE + (z + k) % SIDE + 16 * s]
                    pack_a[k, j, s] = from_a[j][index]
                else:
                    source = (z - j + SIDE) % SIDE
                    index = meta_s[source, y, 0, ((y + k) % SIDE) * SIDE + z + 16 * s]
                    pack_b[k, j, s] = from_b[j][index]

    def send(h, j):
        for k in (2, 1, 3, 0):
            slot_copy(h, k, j).start()

    fill(0, 0)
    send(0, 0)
    fill(1, 0)
    send(1, 0)

    def late(b, carry):
        forward(b)
        return carry

    lax.fori_loop(n_blocks - LAG, n_blocks, late, 0)

    fill(0, 1)
    send(0, 1)
    fill(1, 1)
    send(1, 1)
    fill(0, 3)
    fill(1, 3)

    def passed(b, carry):
        for way in (0, 1):
            pass_copy(0, way, b).wait_recv()
            pass_copy(1, way, b).wait_recv()
        return carry

    lax.fori_loop(0, n_blocks, passed, 0)
    fill(0, 2)
    fill(1, 2)

    def wait_rows(i, carry):
        rows_copy(i).wait()
        return carry

    lax.fori_loop(1, n_dest, wait_rows, 0)
    total = rows[0]
    for i in range(1, n_dest):
        total += rows[i]
    factor = row_target[...] / total
    upright = jnp.transpose(jnp.concatenate([factor, jnp.zeros((S_T - tro, S_T), F32)], axis=0))
    for r in range(tro):
        weights[r] = jnp.broadcast_to(upright[:, r : r + 1], (S_T, S_T))

    col_of = lax.broadcasted_iota(I32, (trd, S_T), 0)

    def line_cols(i, carry):
        s = i % CAP
        sums = list(carry)
        for j in range(SIDE):
            for h in (0, 1):
                for k in range(SIDE):
                    if h == 0:
                        cell = meta_s[z, (y - j + SIDE) % SIDE, 0, y * SIDE + (z + k) % SIDE + 16 * (2 + s)]
                        slot = pack_a[k, j, s]
                    else:
                        cell = meta_s[(z - j + SIDE) % SIDE, y, 0, ((y + k) % SIDE) * SIDE + z + 16 * (2 + s)]
                        slot = pack_b[k, j, s]
                    weight = weights[jnp.minimum(cell // trd, tro - 1), h * HALF : (h + 1) * HALF]
                    line = jnp.sum(weight * slot, axis=0, keepdims=True)
                    column = jnp.where(cell < tro * trd, cell % trd, trd)
                    sums[h * SIDE + k] += jnp.where(col_of == column, line, 0.0)
        return tuple(sums)

    nothing = jnp.zeros((trd, S_T), F32)
    sums = lax.fori_loop(0, CAP, line_cols, (nothing,) * (2 * SIDE))
    for k in range(SIDE):
        cols_a[k] = sums[k]
        cols_b[k] = sums[SIDE + k]

    def cols_copy(h, k):
        held, along = (cols_a, along_z(k)) if h == 0 else (cols_b, along_y(k))
        return remote(held.at[k], held.at[SIDE + k], cols_send.at[h, k - 1], cols_recv.at[h, k - 1], along)

    for k in (2, 1, 3):
        cols_copy(0, k).start()
        cols_copy(1, k).start()
    send(0, 3)
    send(1, 3)
    send(0, 2)
    send(1, 2)

    def prior_cols(r, carry):
        at = pl.multiple_of(r * S_T, S_T)
        weight = weights[r]
        lines = [
            jnp.sum(weight * table[pl.ds(at, S_T), c * S_T : (c + 1) * S_T], axis=0, keepdims=True)
            for c in range(trd)
        ]
        return carry + jnp.concatenate(lines, axis=0)

    wide = lax.fori_loop(0, tro, prior_cols, jnp.zeros((trd, S_T), F32))

    wide += cols_a[0] + cols_b[0]
    for k in range(1, SIDE):
        cols_copy(0, k).wait()
        cols_copy(1, k).wait()
        wide += cols_a[SIDE + k] + cols_b[SIDE + k]
    cols_all[o] = wide

    def cols_o(k):
        return remote(cols_all.at[o], cols_all.at[o], orig_send.at[k - 1], orig_recv.at[k - 1], along_o(k))

    for k in range(1, n_orig):
        cols_o(k).start()
    for k in range(1, n_orig):
        cols_o(k).wait()
    total = cols_all[0]
    for i in range(1, n_orig):
        total += cols_all[i]
    col_factor[...] = col_target[...] / total

    def scale(r, carry):
        at = pl.multiple_of(r * S_T, S_T)
        for c in range(trd):
            columns = slice(c * S_T, (c + 1) * S_T)
            table[pl.ds(at, S_T), columns] = weights[r] * table[pl.ds(at, S_T), columns] * col_factor[c : c + 1, :]
        return carry

    lax.fori_loop(0, tro, scale, 0)

    def sent(b, carry):
        for h in (0, 1):
            for way, k in ((0, 1), (1, 3)):
                gather_copy(h, k, b).wait_send()
                pass_copy(h, way, b).wait_send()
        return carry

    lax.fori_loop(0, n_blocks, sent, 0)
    for j in (0, 1, 3, 2):
        for k in (0, 1, 3, 2):
            slot_copy(0, k, j).wait()
            slot_copy(1, k, j).wait()


def place_kernel(meta, weights, col_factor, slots_a, slots_b, table_in, out, table, out_sem):
    trd = table.shape[1] // S_T
    tro = table.shape[0] // S_T
    me = lax.axis_index("dest")

    def add(i, carry):
        ys = i // SIDE
        zs = i % SIDE
        for s in range(CAP):
            cell = meta[zs, ys, 0, me + 16 * (2 + s)]

            @pl.when(cell < tro * trd)
            def _():
                row = cell // trd
                at = pl.multiple_of(row * S_T, S_T)
                col = pl.multiple_of((cell % trd) * S_T, S_T)
                across = col_factor[pl.ds(cell % trd, 1), :]
                table[pl.ds(at, HALF), pl.ds(col, S_T)] += weights[row, :HALF] * slots_a[zs, ys, s] * across
                table[pl.ds(at + HALF, HALF), pl.ds(col, S_T)] += weights[row, HALF:] * slots_b[ys, zs, s] * across

        return carry

    lax.fori_loop(0, SIDE * SIDE, add, 0)

    def out_copy(r):
        at = pl.multiple_of(r * S_T, S_T)
        return pltpu.make_async_copy(table.at[pl.ds(at, S_T)], out.at[pl.ds(at, S_T)], out_sem.at[r])

    for r in range(tro):
        out_copy(r).start()
    for r in range(tro):
        out_copy(r).wait()


def shards(
    root_blocks,
    sector_map,
    dest_owner,
    local_row,
    local_col,
    present,
    prior,
    row_target,
    col_target,
):
    n_blocks, n_root, _ = root_blocks.shape
    rows_here, cols_here = prior.shape
    tro = rows_here // S_T
    trd = cols_here // S_T
    n_orig = lax.axis_size("orig")
    n_dest = lax.axis_size("dest")
    vmem = pl.BlockSpec(memory_space=pltpu.VMEM)
    smem = pl.BlockSpec(memory_space=pltpu.SMEM)
    hbm = pl.BlockSpec(memory_space=pltpu.HBM)
    dma = pltpu.SemaphoreType.DMA
    got = jax.ShapeDtypeStruct((SIDE, SIDE, CAP, HALF, S_T), F32)
    got_a, got_b, meta, weights, table, col_factor = pl.pallas_call(
        route_kernel,
        out_shape=(
            got,
            got,
            jax.ShapeDtypeStruct((SIDE, SIDE, 1, S_T), I32),
            jax.ShapeDtypeStruct((tro, S_T, S_T), F32),
            jax.ShapeDtypeStruct((rows_here, cols_here), F32),
            jax.ShapeDtypeStruct((trd, S_T), F32),
        ),
        in_specs=[hbm] * 9,
        out_specs=(vmem,) * 6,
        scratch_shapes=[
            pltpu.VMEM((n_root // S_T, S_T), I32),
            *[pltpu.SMEM((1, n_blocks), I32)] * 4,
            pltpu.VMEM((tro, S_T), F32),
            pltpu.VMEM((trd, S_T), F32),
            pltpu.VMEM((n_blocks, n_root, n_root), jnp.bfloat16),
            pltpu.VMEM((S_T, n_root), jnp.bfloat16),
            *[pltpu.VMEM((n_blocks, HALF, S_T), F32)] * (2 * SIDE),
            pltpu.VMEM((SIDE, SIDE, CAP, HALF, S_T), F32),
            pltpu.VMEM((SIDE, SIDE, CAP, HALF, S_T), F32),
            pltpu.VMEM((SIDE, SIDE, 1, S_T), I32),
            pltpu.SMEM((SIDE, SIDE, 1, S_T), I32),
            pltpu.VMEM((S_T, S_T), F32),
            pltpu.VMEM((n_dest, tro, S_T), F32),
            pltpu.VMEM((2 * SIDE, trd, S_T), F32),
            pltpu.VMEM((2 * SIDE, trd, S_T), F32),
            pltpu.VMEM((n_orig, trd, S_T), F32),
            dma((7,)),
            dma((n_blocks,)),
            dma,
            dma,
            dma((2, SIDE - 1, n_blocks)),
            dma((2, SIDE - 1, n_blocks)),
            dma((2, 2, n_blocks)),
            dma((2, 2, n_blocks)),
            dma((2, SIDE - 1, SIDE)),
            dma((2, SIDE - 1, SIDE)),
            dma((2, SIDE)),
            dma((2, SIDE - 1)),
            dma((2, SIDE - 1)),
            dma((n_dest - 1,)),
            dma((n_dest - 1,)),
            dma((2, SIDE - 1)),
            dma((2, SIDE - 1)),
            dma((n_orig - 1,)),
            dma((n_orig - 1,)),
        ],
        compiler_params=pltpu.CompilerParams(
            collective_id=0, has_side_effects=True, vmem_limit_bytes=40 << 20
        ),
        name="route",
    )(*[pltpu.with_memory_space_constraint(x, pltpu.HBM) for x in (
        sector_map.reshape(n_root // S_T, S_T),
        dest_owner.reshape(1, n_blocks),
        local_row.reshape(1, n_blocks),
        local_col.reshape(1, n_blocks),
        present.reshape(1, n_blocks),
        row_target.reshape(tro, S_T),
        col_target.reshape(trd, S_T),
        root_blocks,
        prior,)]
    )
    out, _ = pl.pallas_call(
        place_kernel,
        out_shape=(
            jax.ShapeDtypeStruct((rows_here, cols_here), F32),
            jax.ShapeDtypeStruct((rows_here, cols_here), F32),
        ),
        in_specs=[smem, vmem, vmem, vmem, vmem, vmem],
        out_specs=(hbm, vmem),
        scratch_shapes=[dma((tro,))],
        input_output_aliases={5: 1},
        compiler_params=pltpu.CompilerParams(vmem_limit_bytes=8 << 20),
        name="place",
    )(meta, weights, col_factor, got_a, got_b, table)
    return out


def solution(mesh):
    placed = (
        P(("orig", "dest"), None, None),
        P(),
        P(("orig", "dest"), None),
        P(("orig", "dest")),
        P(("orig", "dest")),
        P(("orig", "dest")),
        P("orig", "dest"),
        P("orig"),
        P("dest"),
    )
    return jax.shard_map(
        shards, mesh=mesh, in_specs=placed, out_specs=P("orig", "dest"), check_vma=False
    )
```

```python
import functools

import jax
import jax.numpy as jnp
from jax import lax
from jax.experimental import pallas as pl
from jax.experimental.pallas import tpu as pltpu
from jax.sharding import PartitionSpec as P

S_T = 128
HALF = S_T // 2
CAP = 2
SIDE = 4
LAG = 6
MESH = pl.DeviceIdType.MESH
NT = (((1,), (1,)), ((), ()))
F32 = jnp.float32
I32 = jnp.int32


def split(x):
    high = x.astype(jnp.bfloat16)
    return high, (x - high.astype(F32)).astype(jnp.bfloat16)


def route_kernel(
    sector_hbm,
    owner_hbm,
    local_row_hbm,
    local_col_hbm,
    present_hbm,
    row_target_hbm,
    col_target_hbm,
    root,
    prior,
    got_a,
    got_b,
    meta_out,
    weights,
    table,
    col_factor,
    sector_ref,
    owner,
    local_row,
    local_col,
    present,
    row_target,
    col_target,
    raw,
    concord_t,
    a_0,
    a_1,
    a_2,
    a_3,
    b_0,
    b_1,
    b_2,
    b_3,
    pack_a,
    pack_b,
    meta_v,
    meta_s,
    row_acc,
    rows,
    parts,
    cols,
    cols_all,
    small_sem,
    raw_sem,
    table_sem,
    meta_sem,
    gather_send,
    gather_recv,
    pass_send,
    pass_recv,
    slot_send,
    slot_recv,
    keep_sem,
    small_send,
    small_recv,
    rows_send,
    rows_recv,
    cols_send,
    cols_recv,
    orig_send,
    orig_recv,
):
    from_a = (a_0, a_1, a_2, a_3)
    from_b = (b_0, b_1, b_2, b_3)
    n_blocks = root.shape[0]
    n_root = root.shape[1]
    n_orig = lax.axis_size("orig")
    n_dest = lax.axis_size("dest")
    tro = table.shape[0] // S_T
    trd = table.shape[1] // S_T
    o = lax.axis_index("orig")
    d = lax.axis_index("dest")
    y = d // SIDE
    z = d % SIDE

    def along_y(k):
        return (o, ((y + k) % SIDE) * SIDE + z)

    def along_z(k):
        return (o, y * SIDE + (z + k) % SIDE)

    def along_d(i):
        return (o, (d + i) % n_dest)

    def along_o(k):
        return ((o + k) % n_orig, d)

    def remote(src, dst, send, recv, device):
        return pltpu.make_async_remote_copy(
            src_ref=src, dst_ref=dst, send_sem=send, recv_sem=recv, device_id=device, device_id_type=MESH
        )

    def raw_copy(b):
        return pltpu.make_async_copy(root.at[b], raw.at[b], raw_sem.at[b])

    loads = [
        pltpu.make_async_copy(src, dst, small_sem.at[i])
        for i, (src, dst) in enumerate(
            (
                (sector_hbm, sector_ref),
                (owner_hbm, owner),
                (local_row_hbm, local_row),
                (local_col_hbm, local_col),
                (present_hbm, present),
                (row_target_hbm, row_target),
                (col_target_hbm, col_target),
            )
        )
    ]
    for load in loads:
        load.start()

    def start_raw(b, carry):
        raw_copy(b).start()
        return carry

    lax.fori_loop(0, n_blocks, start_raw, 0)
    table_copy = pltpu.make_async_copy(prior, table, table_sem)

    barrier = pltpu.get_barrier_semaphore()
    for k in range(1, SIDE):
        pl.semaphore_signal(barrier, inc=1, device_id=along_y(k), device_id_type=MESH)
        pl.semaphore_signal(barrier, inc=1, device_id=along_z(k), device_id_type=MESH)
    for k in range(1, n_orig):
        pl.semaphore_signal(barrier, inc=1, device_id=along_o(k), device_id_type=MESH)

    loads[0].wait()

    target = lax.broadcasted_iota(I32, (S_T, S_T), 0)
    for c in range(n_root // S_T):
        concord_t[:, c * S_T : (c + 1) * S_T] = (target == sector_ref[c : c + 1, :]).astype(F32).astype(jnp.bfloat16)

    for load in loads[1:]:
        load.wait()

    lane = lax.broadcasted_iota(I32, (1, S_T), 1)
    to = lane % 16
    kind = lane // 16
    none = jnp.full((1, S_T), tro * trd, I32)
    first = jnp.zeros((1, S_T), I32)
    second = jnp.zeros((1, S_T), I32)
    cell_1 = none
    cell_2 = none
    for b in reversed(range(n_blocks)):
        hit = to == owner[0, b]
        second = jnp.where(hit, first, second)
        cell_2 = jnp.where(hit, cell_1, cell_2)
        first = jnp.where(hit, b, first)
        cell_1 = jnp.where(hit, local_row[0, b] * trd + local_col[0, b], cell_1)
    meta_v[z, y] = jnp.where(kind == 0, first, jnp.where(kind == 1, second, jnp.where(kind == 2, cell_1, cell_2)))

    pl.semaphore_wait(barrier, 2 * (SIDE - 1) + n_orig - 1)

    def small(i, k, src, dst, device):
        return remote(src, dst, small_send.at[i, k - 1], small_recv.at[i, k - 1], device)

    def meta_y(k):
        return small(0, k, meta_v.at[z, y], meta_v.at[z, y], along_y(k))

    def meta_z(k):
        return small(1, k, meta_v.at[z], meta_v.at[z], along_z(k))

    for k in range(1, SIDE):
        meta_y(k).start()

    def gather_copy(h, k, b):
        held, device = (from_a, along_y(k)) if h == 0 else (from_b, along_z(k))
        return remote(held[0].at[b], held[k].at[b], gather_send.at[h, k - 1, b], gather_recv.at[h, k - 1, b], device)

    def pass_copy(h, way, b):
        held = from_a if h == 0 else from_b
        along = along_y if h == 0 else along_z
        piece = pl.ds(0, HALF // 2) if way == 0 else pl.ds(HALF // 2, HALF // 2)
        source, k = (1, 1) if way == 0 else (3, 3)
        return remote(
            held[source].at[b, piece],
            held[2].at[b, piece],
            pass_send.at[h, way, b],
            pass_recv.at[h, way, b],
            along(k),
        )

    def forward(b):
        for way, k in ((0, 1), (1, 3)):
            for h in (0, 1):
                gather_copy(h, k, b).wait_recv()
                pass_copy(h, way, b).start()

    lanes = lax.broadcasted_iota(I32, (S_T, S_T), 1)

    def halves(b):
        raw_copy(b).wait()
        left = jnp.dot(concord_t[...], raw[b], preferred_element_type=F32)
        return jnp.concatenate(split(left), axis=0)

    def finish(b, stacked):
        both = lax.dot_general(stacked, concord_t[...], NT, preferred_element_type=F32)
        block = (both[:S_T] + both[S_T:]) * present[0, b].astype(F32)
        a_0[b] = block[:HALF]
        b_0[b] = block[HALF:]
        for k in (1, 3):
            gather_copy(0, k, b).start()
            gather_copy(1, k, b).start()

    def aggregate(i, carry):
        low = halves(2 * i)
        high = halves(2 * i + 1)
        finish(2 * i, low)
        finish(2 * i + 1, high)

        @pl.when(i == n_blocks // 2 - 2)
        def _():
            table_copy.start()

        @pl.when(i >= LAG // 2)
        def _():
            forward(2 * i - LAG)
            forward(2 * i - LAG + 1)

        @pl.when(i == 1)
        def _():
            for k in range(1, SIDE):
                meta_y(k).wait()
            for k in range(1, SIDE):
                meta_z(k).start()

        return carry

    lax.fori_loop(0, n_blocks // 2, aggregate, 0)

    upper = jnp.zeros((HALF, S_T), F32)
    lower = jnp.zeros((HALF, S_T), F32)
    for b in range(n_blocks):
        here = lanes[:HALF] == local_row[0, b]
        upper += jnp.where(here, jnp.sum(a_0[b], axis=1, keepdims=True), 0.0)
        lower += jnp.where(here, jnp.sum(b_0[b], axis=1, keepdims=True), 0.0)
    row_acc[:HALF] = upper
    row_acc[HALF:] = lower

    table_copy.wait()

    def prior_rows(r, carry):
        at = pl.multiple_of(r * S_T, S_T)
        tile = table[pl.ds(at, S_T), 0:S_T]
        for c in range(1, trd):
            tile += table[pl.ds(at, S_T), c * S_T : (c + 1) * S_T]
        row_acc[...] += jnp.where(lanes == r, jnp.sum(tile, axis=1, keepdims=True), 0.0)
        return carry

    lax.fori_loop(0, tro, prior_rows, 0)
    rows[d] = jnp.transpose(row_acc[...])[:tro]

    def rows_copy(i):
        return remote(rows.at[d], rows.at[d], rows_send.at[i - 1], rows_recv.at[i - 1], along_d(i))

    def start_rows(i, carry):
        rows_copy(i).start()
        return carry

    lax.fori_loop(1, n_dest, start_rows, 0)

    for k in range(1, SIDE):
        meta_z(k).wait()
    meta_copy = pltpu.make_async_copy(meta_v, meta_s, meta_sem)
    meta_copy.start()
    meta_copy.wait()
    meta_out[...] = meta_v[...]

    def slot_copy(h, k, j):
        if h == 0:
            src, dst, device = pack_a.at[k, j], got_a.at[z, (y - j + SIDE) % SIDE], along_z(k)
        else:
            src, dst, device = pack_b.at[k, j], got_b.at[y, (z - j + SIDE) % SIDE], along_y(k)
        if k == 0:
            return pltpu.make_async_copy(src, dst, keep_sem.at[h, j])
        return remote(src, dst, slot_send.at[h, k - 1, j], slot_recv.at[h, k - 1, j], device)

    def fill(h, j):
        for k in (2, 1, 3, 0):
            for s in range(CAP):
                if h == 0:
                    source = (y - j + SIDE) % SIDE
                    index = meta_s[z, source, 0, y * SIDE + (z + k) % SIDE + 16 * s]
                    pack_a[k, j, s] = from_a[j][index]
                else:
                    source = (z - j + SIDE) % SIDE
                    index = meta_s[source, y, 0, ((y + k) % SIDE) * SIDE + z + 16 * s]
                    pack_b[k, j, s] = from_b[j][index]

    def send(h, j):
        for k in (2, 1, 3, 0):
            slot_copy(h, k, j).start()

    fill(0, 0)
    send(0, 0)
    fill(1, 0)
    send(1, 0)

    def late(b, carry):
        forward(b)
        return carry

    lax.fori_loop(n_blocks - LAG, n_blocks, late, 0)

    fill(0, 1)
    send(0, 1)
    fill(1, 1)
    def wait_rows(i, carry):
        rows_copy(i).wait()
        return carry

    lax.fori_loop(1, n_dest, wait_rows, 0)
    total = rows[0]
    for i in range(1, n_dest):
        total += rows[i]
    factor = row_target[...] / total
    upright = jnp.transpose(jnp.concatenate([factor, jnp.zeros((S_T - tro, S_T), F32)], axis=0))
    for r in range(tro):
        weights[r] = jnp.broadcast_to(upright[:, r : r + 1], (S_T, S_T))

    place = lax.broadcasted_iota(I32, parts.shape, 0) * trd + lax.broadcasted_iota(I32, parts.shape, 1)
    spread = jnp.zeros(parts.shape, F32)
    for b in range(n_blocks):
        weight = weights[local_row[0, b]]
        line = jnp.sum(weight[:HALF] * a_0[b] + weight[HALF:] * b_0[b], axis=0, keepdims=True)
        here = place == owner[0, b] * trd + local_col[0, b]
        spread += jnp.where(here, jnp.broadcast_to(line[None], parts.shape), 0.0)
    parts[...] = spread
    cols[d] = parts[d]

    def cols_copy(i):
        return remote(parts.at[(d + i) % n_dest], cols.at[d], cols_send.at[i - 1], cols_recv.at[i - 1], along_d(i))

    def start_cols(i, carry):
        cols_copy(i).start()
        return carry

    lax.fori_loop(1, n_dest, start_cols, 0)
    send(1, 1)
    fill(0, 3)
    send(0, 3)
    fill(1, 3)
    send(1, 3)

    def prior_cols(r, carry):
        at = pl.multiple_of(r * S_T, S_T)
        weight = weights[r]
        lines = []
        for c in range(trd):
            columns = slice(c * S_T, (c + 1) * S_T)
            scaled = weight * table[pl.ds(at, S_T), columns]
            table[pl.ds(at, S_T), columns] = scaled
            lines.append(jnp.sum(scaled, axis=0, keepdims=True))
        return carry + jnp.concatenate(lines, axis=0)

    wide = lax.fori_loop(0, tro, prior_cols, jnp.zeros((trd, S_T), F32))

    def passed(b, carry):
        for way in (0, 1):
            pass_copy(0, way, b).wait_recv()
            pass_copy(1, way, b).wait_recv()
        return carry

    lax.fori_loop(0, n_blocks, passed, 0)
    fill(0, 2)
    send(0, 2)
    fill(1, 2)
    send(1, 2)

    def wait_cols(i, carry):
        cols_copy(i).wait()
        return carry

    lax.fori_loop(1, n_dest, wait_cols, 0)
    for i in range(n_dest):
        wide += cols[i]
    cols_all[o] = wide

    def cols_o(k):
        return remote(cols_all.at[o], cols_all.at[o], orig_send.at[k - 1], orig_recv.at[k - 1], along_o(k))

    for k in range(1, n_orig):
        cols_o(k).start()

    def sent(b, carry):
        for h in (0, 1):
            for way, k in ((0, 1), (1, 3)):
                gather_copy(h, k, b).wait_send()
                pass_copy(h, way, b).wait_send()
        return carry

    lax.fori_loop(0, n_blocks, sent, 0)
    for j in (0, 1, 3, 2):
        for k in (0, 1, 3, 2):
            slot_copy(0, k, j).wait()
            slot_copy(1, k, j).wait()

    for k in range(1, n_orig):
        cols_o(k).wait()
    total = cols_all[0]
    for i in range(1, n_orig):
        total += cols_all[i]
    col_factor[...] = col_target[...] / total


def place_kernel(meta, weights, col_factor, slots_a, slots_b, table_in, out, table, out_sem):
    trd = table.shape[1] // S_T
    tro = table.shape[0] // S_T
    me = lax.axis_index("dest")

    def add(i, carry):
        ys = i // SIDE
        zs = i % SIDE
        for s in range(CAP):
            cell = meta[zs, ys, 0, me + 16 * (2 + s)]

            @pl.when(cell < tro * trd)
            def _():
                row = cell // trd
                at = pl.multiple_of(row * S_T, S_T)
                col = pl.multiple_of((cell % trd) * S_T, S_T)
                table[pl.ds(at, HALF), pl.ds(col, S_T)] += weights[row, :HALF] * slots_a[zs, ys, s]
                table[pl.ds(at + HALF, HALF), pl.ds(col, S_T)] += weights[row, HALF:] * slots_b[ys, zs, s]

        return carry

    lax.fori_loop(0, SIDE * SIDE, add, 0)

    def out_copy(r):
        at = pl.multiple_of(r * S_T, S_T)
        return pltpu.make_async_copy(table.at[pl.ds(at, S_T)], out.at[pl.ds(at, S_T)], out_sem.at[r])

    for r in range(tro):
        for c in range(trd):
            where = (slice(r * S_T, (r + 1) * S_T), slice(c * S_T, (c + 1) * S_T))
            table[where] = table[where] * col_factor[c : c + 1, :]
        out_copy(r).start()
    for r in range(tro):
        out_copy(r).wait()


def shards(
    root_blocks,
    sector_map,
    dest_owner,
    local_row,
    local_col,
    present,
    prior,
    row_target,
    col_target,
):
    n_blocks, n_root, _ = root_blocks.shape
    rows_here, cols_here = prior.shape
    tro = rows_here // S_T
    trd = cols_here // S_T
    n_orig = lax.axis_size("orig")
    n_dest = lax.axis_size("dest")
    vmem = pl.BlockSpec(memory_space=pltpu.VMEM)
    smem = pl.BlockSpec(memory_space=pltpu.SMEM)
    hbm = pl.BlockSpec(memory_space=pltpu.HBM)
    dma = pltpu.SemaphoreType.DMA
    got = jax.ShapeDtypeStruct((SIDE, SIDE, CAP, HALF, S_T), F32)
    got_a, got_b, meta, weights, table, col_factor = pl.pallas_call(
        route_kernel,
        out_shape=(
            got,
            got,
            jax.ShapeDtypeStruct((SIDE, SIDE, 1, S_T), I32),
            jax.ShapeDtypeStruct((tro, S_T, S_T), F32),
            jax.ShapeDtypeStruct((rows_here, cols_here), F32),
            jax.ShapeDtypeStruct((trd, S_T), F32),
        ),
        in_specs=[hbm] * 9,
        out_specs=(vmem,) * 6,
        scratch_shapes=[
            pltpu.VMEM((n_root // S_T, S_T), I32),
            *[pltpu.SMEM((1, n_blocks), I32)] * 4,
            pltpu.VMEM((tro, S_T), F32),
            pltpu.VMEM((trd, S_T), F32),
            pltpu.VMEM((n_blocks, n_root, n_root), jnp.bfloat16),
            pltpu.VMEM((S_T, n_root), jnp.bfloat16),
            *[pltpu.VMEM((n_blocks, HALF, S_T), F32)] * (2 * SIDE),
            pltpu.VMEM((SIDE, SIDE, CAP, HALF, S_T), F32),
            pltpu.VMEM((SIDE, SIDE, CAP, HALF, S_T), F32),
            pltpu.VMEM((SIDE, SIDE, 1, S_T), I32),
            pltpu.SMEM((SIDE, SIDE, 1, S_T), I32),
            pltpu.VMEM((S_T, S_T), F32),
            pltpu.VMEM((n_dest, tro, S_T), F32),
            pltpu.VMEM((n_dest, trd, S_T), F32),
            pltpu.VMEM((n_dest, trd, S_T), F32),
            pltpu.VMEM((n_orig, trd, S_T), F32),
            dma((7,)),
            dma((n_blocks,)),
            dma,
            dma,
            dma((2, SIDE - 1, n_blocks)),
            dma((2, SIDE - 1, n_blocks)),
            dma((2, 2, n_blocks)),
            dma((2, 2, n_blocks)),
            dma((2, SIDE - 1, SIDE)),
            dma((2, SIDE - 1, SIDE)),
            dma((2, SIDE)),
            dma((2, SIDE - 1)),
            dma((2, SIDE - 1)),
            dma((n_dest - 1,)),
            dma((n_dest - 1,)),
            dma((n_dest - 1,)),
            dma((n_dest - 1,)),
            dma((n_orig - 1,)),
            dma((n_orig - 1,)),
        ],
        compiler_params=pltpu.CompilerParams(
            collective_id=0, has_side_effects=True, vmem_limit_bytes=40 << 20
        ),
        name="route",
    )(*[pltpu.with_memory_space_constraint(x, pltpu.HBM) for x in (
        sector_map.reshape(n_root // S_T, S_T),
        dest_owner.reshape(1, n_blocks),
        local_row.reshape(1, n_blocks),
        local_col.reshape(1, n_blocks),
        present.reshape(1, n_blocks),
        row_target.reshape(tro, S_T),
        col_target.reshape(trd, S_T),
        root_blocks,
        prior,)]
    )
    out, _ = pl.pallas_call(
        place_kernel,
        out_shape=(
            jax.ShapeDtypeStruct((rows_here, cols_here), F32),
            jax.ShapeDtypeStruct((rows_here, cols_here), F32),
        ),
        in_specs=[smem, vmem, vmem, vmem, vmem, vmem],
        out_specs=(hbm, vmem),
        scratch_shapes=[dma((tro,))],
        input_output_aliases={5: 1},
        compiler_params=pltpu.CompilerParams(vmem_limit_bytes=8 << 20),
        name="place",
    )(meta, weights, col_factor, got_a, got_b, table)
    return out


def solution(mesh):
    placed = (
        P(("orig", "dest"), None, None),
        P(),
        P(("orig", "dest"), None),
        P(("orig", "dest")),
        P(("orig", "dest")),
        P(("orig", "dest")),
        P("orig", "dest"),
        P("orig"),
        P("dest"),
    )
    return jax.shard_map(
        shards, mesh=mesh, in_specs=placed, out_specs=P("orig", "dest"), check_vma=False
    )
```

```python
import functools

import jax
import jax.numpy as jnp
from jax import lax
from jax.experimental import pallas as pl
from jax.experimental.pallas import tpu as pltpu
from jax.sharding import PartitionSpec as P

S_T = 128
HALF = S_T // 2
CAP = 2
SIDE = 4
LAG = 4
MESH = pl.DeviceIdType.MESH
NT = (((1,), (1,)), ((), ()))
F32 = jnp.float32
I32 = jnp.int32


def split(x):
    high = x.astype(jnp.bfloat16)
    return high, (x - high.astype(F32)).astype(jnp.bfloat16)


def route_kernel(
    sector_hbm,
    owner_hbm,
    local_row_hbm,
    local_col_hbm,
    present_hbm,
    row_target_hbm,
    col_target_hbm,
    root,
    prior,
    got_a,
    got_b,
    meta_out,
    weights,
    table,
    col_factor,
    sector_ref,
    owner,
    local_row,
    local_col,
    present,
    row_target,
    col_target,
    raw,
    concord_t,
    a_0,
    a_1,
    a_2,
    a_3,
    b_0,
    b_1,
    b_2,
    b_3,
    pack_a,
    pack_b,
    meta_v,
    meta_s,
    row_acc,
    rows,
    parts,
    cols,
    cols_all,
    small_sem,
    raw_sem,
    table_sem,
    meta_sem,
    gather_send,
    gather_recv,
    pass_send,
    pass_recv,
    slot_send,
    slot_recv,
    keep_sem,
    small_send,
    small_recv,
    rows_send,
    rows_recv,
    cols_send,
    cols_recv,
    orig_send,
    orig_recv,
):
    from_a = (a_0, a_1, a_2, a_3)
    from_b = (b_0, b_1, b_2, b_3)
    n_blocks = root.shape[0]
    n_root = root.shape[1]
    n_orig = lax.axis_size("orig")
    n_dest = lax.axis_size("dest")
    tro = table.shape[0] // S_T
    trd = table.shape[1] // S_T
    o = lax.axis_index("orig")
    d = lax.axis_index("dest")
    y = d // SIDE
    z = d % SIDE

    def along_y(k):
        return (o, ((y + k) % SIDE) * SIDE + z)

    def along_z(k):
        return (o, y * SIDE + (z + k) % SIDE)

    def along_d(i):
        return (o, (d + i) % n_dest)

    def along_o(k):
        return ((o + k) % n_orig, d)

    def remote(src, dst, send, recv, device):
        return pltpu.make_async_remote_copy(
            src_ref=src, dst_ref=dst, send_sem=send, recv_sem=recv, device_id=device, device_id_type=MESH
        )

    def raw_copy(b):
        return pltpu.make_async_copy(root.at[b], raw.at[b], raw_sem.at[b])

    loads = [
        pltpu.make_async_copy(src, dst, small_sem.at[i])
        for i, (src, dst) in enumerate(
            (
                (sector_hbm, sector_ref),
                (owner_hbm, owner),
                (local_row_hbm, local_row),
                (local_col_hbm, local_col),
                (present_hbm, present),
                (row_target_hbm, row_target),
                (col_target_hbm, col_target),
            )
        )
    ]
    for load in loads:
        load.start()

    def start_raw(b, carry):
        raw_copy(b).start()
        return carry

    lax.fori_loop(0, n_blocks, start_raw, 0)
    table_copy = pltpu.make_async_copy(prior, table, table_sem)

    barrier = pltpu.get_barrier_semaphore()
    for k in range(1, SIDE):
        pl.semaphore_signal(barrier, inc=1, device_id=along_y(k), device_id_type=MESH)
        pl.semaphore_signal(barrier, inc=1, device_id=along_z(k), device_id_type=MESH)
    for k in range(1, n_orig):
        pl.semaphore_signal(barrier, inc=1, device_id=along_o(k), device_id_type=MESH)

    loads[0].wait()

    target = lax.broadcasted_iota(I32, (S_T, S_T), 0)
    for c in range(n_root // S_T):
        concord_t[:, c * S_T : (c + 1) * S_T] = (target == sector_ref[c : c + 1, :]).astype(F32).astype(jnp.bfloat16)

    for load in loads[1:]:
        load.wait()

    lane = lax.broadcasted_iota(I32, (1, S_T), 1)
    to = lane % 16
    kind = lane // 16
    none = jnp.full((1, S_T), tro * trd, I32)
    first = jnp.zeros((1, S_T), I32)
    second = jnp.zeros((1, S_T), I32)
    cell_1 = none
    cell_2 = none
    for b in reversed(range(n_blocks)):
        hit = to == owner[0, b]
        second = jnp.where(hit, first, second)
        cell_2 = jnp.where(hit, cell_1, cell_2)
        first = jnp.where(hit, b, first)
        cell_1 = jnp.where(hit, local_row[0, b] * trd + local_col[0, b], cell_1)
    meta_v[z, y] = jnp.where(kind == 0, first, jnp.where(kind == 1, second, jnp.where(kind == 2, cell_1, cell_2)))

    pl.semaphore_wait(barrier, 2 * (SIDE - 1) + n_orig - 1)

    def small(i, k, src, dst, device):
        return remote(src, dst, small_send.at[i, k - 1], small_recv.at[i, k - 1], device)

    def meta_y(k):
        return small(0, k, meta_v.at[z, y], meta_v.at[z, y], along_y(k))

    def meta_z(k):
        return small(1, k, meta_v.at[z], meta_v.at[z], along_z(k))

    for k in range(1, SIDE):
        meta_y(k).start()

    def gather_copy(h, k, b):
        held, device = (from_a, along_y(k)) if h == 0 else (from_b, along_z(k))
        return remote(held[0].at[b], held[k].at[b], gather_send.at[h, k - 1, b], gather_recv.at[h, k - 1, b], device)

    def pass_copy(h, way, b):
        held = from_a if h == 0 else from_b
        along = along_y if h == 0 else along_z
        piece = pl.ds(0, HALF // 2) if way == 0 else pl.ds(HALF // 2, HALF // 2)
        source, k = (1, 1) if way == 0 else (3, 3)
        return remote(
            held[source].at[b, piece],
            held[2].at[b, piece],
            pass_send.at[h, way, b],
            pass_recv.at[h, way, b],
            along(k),
        )

    def forward(b):
        for way, k in ((0, 1), (1, 3)):
            for h in (0, 1):
                gather_copy(h, k, b).wait_recv()
                pass_copy(h, way, b).start()

    lanes = lax.broadcasted_iota(I32, (S_T, S_T), 1)

    def halves(b):
        raw_copy(b).wait()
        left = jnp.dot(concord_t[...], raw[b], preferred_element_type=F32)
        return jnp.concatenate(split(left), axis=0)

    def finish(b, stacked):
        both = lax.dot_general(stacked, concord_t[...], NT, preferred_element_type=F32)
        block = (both[:S_T] + both[S_T:]) * present[0, b].astype(F32)
        a_0[b] = block[:HALF]
        b_0[b] = block[HALF:]
        for k in (1, 3):
            gather_copy(0, k, b).start()
            gather_copy(1, k, b).start()

    def aggregate(i, carry):
        low = halves(2 * i)
        high = halves(2 * i + 1)
        finish(2 * i, low)
        finish(2 * i + 1, high)

        @pl.when(i == n_blocks // 2 - 2)
        def _():
            table_copy.start()

        @pl.when(i >= LAG // 2)
        def _():
            forward(2 * i - LAG)
            forward(2 * i - LAG + 1)

        @pl.when(i == 1)
        def _():
            for k in range(1, SIDE):
                meta_y(k).wait()
            for k in range(1, SIDE):
                meta_z(k).start()

        return carry

    lax.fori_loop(0, n_blocks // 2, aggregate, 0)

    upper = jnp.zeros((HALF, S_T), F32)
    lower = jnp.zeros((HALF, S_T), F32)
    for b in range(n_blocks):
        here = lanes[:HALF] == local_row[0, b]
        upper += jnp.where(here, jnp.sum(a_0[b], axis=1, keepdims=True), 0.0)
        lower += jnp.where(here, jnp.sum(b_0[b], axis=1, keepdims=True), 0.0)
    row_acc[:HALF] = upper
    row_acc[HALF:] = lower

    table_copy.wait()

    def prior_rows(r, carry):
        at = pl.multiple_of(r * S_T, S_T)
        tile = table[pl.ds(at, S_T), 0:S_T]
        for c in range(1, trd):
            tile += table[pl.ds(at, S_T), c * S_T : (c + 1) * S_T]
        row_acc[...] += jnp.where(lanes == r, jnp.sum(tile, axis=1, keepdims=True), 0.0)
        return carry

    lax.fori_loop(0, tro, prior_rows, 0)
    rows[d] = jnp.transpose(row_acc[...])[:tro]

    def rows_copy(i):
        return remote(rows.at[d], rows.at[d], rows_send.at[i - 1], rows_recv.at[i - 1], along_d(i))

    def start_rows(i, carry):
        rows_copy(i).start()
        return carry

    lax.fori_loop(1, n_dest, start_rows, 0)

    for k in range(1, SIDE):
        meta_z(k).wait()
    meta_copy = pltpu.make_async_copy(meta_v, meta_s, meta_sem)
    meta_copy.start()
    meta_copy.wait()
    meta_out[...] = meta_v[...]

    def slot_copy(h, k, j):
        if h == 0:
            src, dst, device = pack_a.at[k, j], got_a.at[z, (y - j + SIDE) % SIDE], along_z(k)
        else:
            src, dst, device = pack_b.at[k, j], got_b.at[y, (z - j + SIDE) % SIDE], along_y(k)
        if k == 0:
            return pltpu.make_async_copy(src, dst, keep_sem.at[h, j])
        return remote(src, dst, slot_send.at[h, k - 1, j], slot_recv.at[h, k - 1, j], device)

    def fill(h, j):
        for k in (2, 1, 3, 0):
            for s in range(CAP):
                if h == 0:
                    source = (y - j + SIDE) % SIDE
                    index = meta_s[z, source, 0, y * SIDE + (z + k) % SIDE + 16 * s]
                    pack_a[k, j, s] = from_a[j][index]
                else:
                    source = (z - j + SIDE) % SIDE
                    index = meta_s[source, y, 0, ((y + k) % SIDE) * SIDE + z + 16 * s]
                    pack_b[k, j, s] = from_b[j][index]

    def send(h, j):
        for k in (1, 3, 2, 0):
            slot_copy(h, k, j).start()

    fill(0, 0)
    send(0, 0)
    fill(1, 0)
    send(1, 0)

    def late(b, carry):
        forward(b)
        return carry

    lax.fori_loop(n_blocks - LAG, n_blocks, late, 0)

    fill(0, 1)
    send(0, 1)
    fill(1, 1)
    def wait_rows(i, carry):
        rows_copy(i).wait()
        return carry

    lax.fori_loop(1, n_dest, wait_rows, 0)
    total = rows[0]
    for i in range(1, n_dest):
        total += rows[i]
    factor = row_target[...] / total
    upright = jnp.transpose(jnp.concatenate([factor, jnp.zeros((S_T - tro, S_T), F32)], axis=0))
    for r in range(tro):
        weights[r] = jnp.broadcast_to(upright[:, r : r + 1], (S_T, S_T))

    place = lax.broadcasted_iota(I32, parts.shape, 0) * trd + lax.broadcasted_iota(I32, parts.shape, 1)
    spread = jnp.zeros(parts.shape, F32)
    for b in range(n_blocks):
        weight = weights[local_row[0, b]]
        line = jnp.sum(weight[:HALF] * a_0[b] + weight[HALF:] * b_0[b], axis=0, keepdims=True)
        here = place == owner[0, b] * trd + local_col[0, b]
        spread += jnp.where(here, jnp.broadcast_to(line[None], parts.shape), 0.0)
    parts[...] = spread
    cols[d] = parts[d]

    def cols_copy(i):
        return remote(parts.at[(d + i) % n_dest], cols.at[d], cols_send.at[i - 1], cols_recv.at[i - 1], along_d(i))

    def start_cols(i, carry):
        cols_copy(i).start()
        return carry

    lax.fori_loop(1, n_dest, start_cols, 0)
    send(1, 1)
    fill(0, 3)
    send(0, 3)
    fill(1, 3)
    send(1, 3)

    def passed(b, carry):
        for way in (0, 1):
            pass_copy(0, way, b).wait_recv()
            pass_copy(1, way, b).wait_recv()
        return carry

    lax.fori_loop(0, n_blocks, passed, 0)
    fill(0, 2)
    send(0, 2)
    fill(1, 2)
    send(1, 2)

    def prior_cols(r, carry):
        at = pl.multiple_of(r * S_T, S_T)
        weight = weights[r]
        lines = []
        for c in range(trd):
            columns = slice(c * S_T, (c + 1) * S_T)
            scaled = weight * table[pl.ds(at, S_T), columns]
            table[pl.ds(at, S_T), columns] = scaled
            lines.append(jnp.sum(scaled, axis=0, keepdims=True))
        return carry + jnp.concatenate(lines, axis=0)

    wide = lax.fori_loop(0, tro, prior_cols, jnp.zeros((trd, S_T), F32))

    def wait_cols(i, carry):
        cols_copy(i).wait()
        return carry

    lax.fori_loop(1, n_dest, wait_cols, 0)
    for i in range(n_dest):
        wide += cols[i]
    cols_all[o] = wide

    def cols_o(k):
        return remote(cols_all.at[o], cols_all.at[o], orig_send.at[k - 1], orig_recv.at[k - 1], along_o(k))

    for k in range(1, n_orig):
        cols_o(k).start()

    def sent(b, carry):
        for h in (0, 1):
            for way, k in ((0, 1), (1, 3)):
                gather_copy(h, k, b).wait_send()
                pass_copy(h, way, b).wait_send()
        return carry

    lax.fori_loop(0, n_blocks, sent, 0)
    for j in (0, 1, 3, 2):
        for k in (0, 1, 3, 2):
            slot_copy(0, k, j).wait()
            slot_copy(1, k, j).wait()

    for k in range(1, n_orig):
        cols_o(k).wait()
    total = cols_all[0]
    for i in range(1, n_orig):
        total += cols_all[i]
    col_factor[...] = col_target[...] / total


def place_kernel(meta, weights, col_factor, slots_a, slots_b, table_in, out, table, out_sem):
    trd = table.shape[1] // S_T
    tro = table.shape[0] // S_T
    me = lax.axis_index("dest")

    def add(i, carry):
        ys = i // SIDE
        zs = i % SIDE
        for s in range(CAP):
            cell = meta[zs, ys, 0, me + 16 * (2 + s)]

            @pl.when(cell < tro * trd)
            def _():
                row = cell // trd
                at = pl.multiple_of(row * S_T, S_T)
                col = pl.multiple_of((cell % trd) * S_T, S_T)
                table[pl.ds(at, HALF), pl.ds(col, S_T)] += weights[row, :HALF] * slots_a[zs, ys, s]
                table[pl.ds(at + HALF, HALF), pl.ds(col, S_T)] += weights[row, HALF:] * slots_b[ys, zs, s]

        return carry

    lax.fori_loop(0, SIDE * SIDE, add, 0)

    def out_copy(r):
        at = pl.multiple_of(r * S_T, S_T)
        return pltpu.make_async_copy(table.at[pl.ds(at, S_T)], out.at[pl.ds(at, S_T)], out_sem.at[r])

    for r in range(tro):
        for c in range(trd):
            where = (slice(r * S_T, (r + 1) * S_T), slice(c * S_T, (c + 1) * S_T))
            table[where] = table[where] * col_factor[c : c + 1, :]
        out_copy(r).start()
    for r in range(tro):
        out_copy(r).wait()


def shards(
    root_blocks,
    sector_map,
    dest_owner,
    local_row,
    local_col,
    present,
    prior,
    row_target,
    col_target,
):
    n_blocks, n_root, _ = root_blocks.shape
    rows_here, cols_here = prior.shape
    tro = rows_here // S_T
    trd = cols_here // S_T
    n_orig = lax.axis_size("orig")
    n_dest = lax.axis_size("dest")
    vmem = pl.BlockSpec(memory_space=pltpu.VMEM)
    smem = pl.BlockSpec(memory_space=pltpu.SMEM)
    hbm = pl.BlockSpec(memory_space=pltpu.HBM)
    dma = pltpu.SemaphoreType.DMA
    got = jax.ShapeDtypeStruct((SIDE, SIDE, CAP, HALF, S_T), F32)
    got_a, got_b, meta, weights, table, col_factor = pl.pallas_call(
        route_kernel,
        out_shape=(
            got,
            got,
            jax.ShapeDtypeStruct((SIDE, SIDE, 1, S_T), I32),
            jax.ShapeDtypeStruct((tro, S_T, S_T), F32),
            jax.ShapeDtypeStruct((rows_here, cols_here), F32),
            jax.ShapeDtypeStruct((trd, S_T), F32),
        ),
        in_specs=[hbm] * 9,
        out_specs=(vmem,) * 6,
        scratch_shapes=[
            pltpu.VMEM((n_root // S_T, S_T), I32),
            *[pltpu.SMEM((1, n_blocks), I32)] * 4,
            pltpu.VMEM((tro, S_T), F32),
            pltpu.VMEM((trd, S_T), F32),
            pltpu.VMEM((n_blocks, n_root, n_root), jnp.bfloat16),
            pltpu.VMEM((S_T, n_root), jnp.bfloat16),
            *[pltpu.VMEM((n_blocks, HALF, S_T), F32)] * (2 * SIDE),
            pltpu.VMEM((SIDE, SIDE, CAP, HALF, S_T), F32),
            pltpu.VMEM((SIDE, SIDE, CAP, HALF, S_T), F32),
            pltpu.VMEM((SIDE, SIDE, 1, S_T), I32),
            pltpu.SMEM((SIDE, SIDE, 1, S_T), I32),
            pltpu.VMEM((S_T, S_T), F32),
            pltpu.VMEM((n_dest, tro, S_T), F32),
            pltpu.VMEM((n_dest, trd, S_T), F32),
            pltpu.VMEM((n_dest, trd, S_T), F32),
            pltpu.VMEM((n_orig, trd, S_T), F32),
            dma((7,)),
            dma((n_blocks,)),
            dma,
            dma,
            dma((2, SIDE - 1, n_blocks)),
            dma((2, SIDE - 1, n_blocks)),
            dma((2, 2, n_blocks)),
            dma((2, 2, n_blocks)),
            dma((2, SIDE - 1, SIDE)),
            dma((2, SIDE - 1, SIDE)),
            dma((2, SIDE)),
            dma((2, SIDE - 1)),
            dma((2, SIDE - 1)),
            dma((n_dest - 1,)),
            dma((n_dest - 1,)),
            dma((n_dest - 1,)),
            dma((n_dest - 1,)),
            dma((n_orig - 1,)),
            dma((n_orig - 1,)),
        ],
        compiler_params=pltpu.CompilerParams(
            collective_id=0, has_side_effects=True, vmem_limit_bytes=40 << 20
        ),
        name="route",
    )(*[pltpu.with_memory_space_constraint(x, pltpu.HBM) for x in (
        sector_map.reshape(n_root // S_T, S_T),
        dest_owner.reshape(1, n_blocks),
        local_row.reshape(1, n_blocks),
        local_col.reshape(1, n_blocks),
        present.reshape(1, n_blocks),
        row_target.reshape(tro, S_T),
        col_target.reshape(trd, S_T),
        root_blocks,
        prior,)]
    )
    out, _ = pl.pallas_call(
        place_kernel,
        out_shape=(
            jax.ShapeDtypeStruct((rows_here, cols_here), F32),
            jax.ShapeDtypeStruct((rows_here, cols_here), F32),
        ),
        in_specs=[smem, vmem, vmem, vmem, vmem, vmem],
        out_specs=(hbm, vmem),
        scratch_shapes=[dma((tro,))],
        input_output_aliases={5: 1},
        compiler_params=pltpu.CompilerParams(vmem_limit_bytes=8 << 20),
        name="place",
    )(meta, weights, col_factor, got_a, got_b, table)
    return out


def solution(mesh):
    placed = (
        P(("orig", "dest"), None, None),
        P(),
        P(("orig", "dest"), None),
        P(("orig", "dest")),
        P(("orig", "dest")),
        P(("orig", "dest")),
        P("orig", "dest"),
        P("orig"),
        P("dest"),
    )
    return jax.shard_map(
        shards, mesh=mesh, in_specs=placed, out_specs=P("orig", "dest"), check_vma=False
    )
```
